32 devices in a mesh: groups: 2 (over x), dp: 16 (over z, y, core).
Axes of the slice: x: 2, y: 2, z: 4, core: 2. Of those that a mesh axis runs over, the one named last changes fastest.
Arguments:
- images: bfloat16 [16, 128, 128, 320], P('groups', 'dp'), parts along dimension 0, may hold values from -6 to 6
- kernel_weights: bfloat16 [16, 2, 3, 3, 320, 320], P('dp'), may hold values from -0.109375 to 0.109375
- kernel_momentum: float32 [16, 2, 3, 3, 320, 320], P('dp'), may hold values from -0.12 to 0.12
- kernel_grads: bfloat16 [16, 2, 3, 3, 320, 320], P('dp'), may hold values from -0.119628906 to 0.119628906
- owners: int32 [2], replicated, may hold values from 0 to 15
Outputs:
- blocks_out: bfloat16 [16, 128, 128, 320], P('groups', 'dp'), parts along dimension 0
The draws below stay inside these ranges and needn't reach their ends.
There are 2 independent parts, one for each index of `groups`. The reference program is written for one: setup_inputs(seed, part) draws one part's arguments, and reference() takes and returns one part's arrays. A program takes and returns all parts, laid end to end along the dimension named above; an argument that names none is the same for every part. Nothing has to cross between parts.
Inputs may be any that keep to these rules, and one draw needn't show every extreme that they name: `owners`: each entry is a slot index along the first dimension of the kernel state.
All inputs are finite; a program needn't handle non-finite values.
Results may differ from the reference program's by a relative error of at most 0.0095.
Values may be sent and summed in bfloat16 or wider, within the bound.
A program may use at most 128 MiB of HBM per device.

```python
import jax
import jax.numpy as jnp
from jax import lax

C = 320
IMGS = 8
WIDTH = 128
HEIGHT = 128
N_DP = 16


def level_of(own_key, dims, shards, low, high):
    level = 1.0
    for axis_at, blocks in shards:
        steps = jax.random.uniform(jax.random.fold_in(jax.random.fold_in(own_key, 6), axis_at), (blocks,), jnp.float32, low / len(shards), high / len(shards))
        level = level * jnp.repeat(jnp.exp(steps), dims[axis_at] // blocks).reshape((-1,) + (1,) * (len(dims) - 1 - axis_at))
    return level


def centred(own_key, dims, scale, most, shards=(), kind=jnp.bfloat16):
    gain = level_of(own_key, dims, shards, -0.22, 0.18) if shards else 1.0
    result = jax.random.normal(own_key, dims, jnp.float32) * scale * gain
    return jnp.minimum(jnp.maximum(result, -most), most).astype(kind)


def setup_inputs(seed: int = 0, part: int = 0) -> dict:
    keys = jax.random.split(jax.random.key(seed), 6)
    part_splits = jax.random.split(jax.random.fold_in(keys[5], part), 6)
    return {
        "images": centred(part_splits[0], (IMGS, HEIGHT, WIDTH, C), 1.0, 6.0, ((1, 16),)),
        "kernel_weights": centred(keys[1], (N_DP, 2, 3, 3, C, C), (9 * C) ** -0.5, 0.109375, ((0, 16),)),
        "kernel_momentum": centred(keys[2], (N_DP, 2, 3, 3, C, C), 0.02, 0.12, ((0, 16),), jnp.float32),
        "kernel_grads": centred(keys[3], (N_DP, 2, 3, 3, C, C), 0.02, 0.119628906, ((0, 16),)),
        "owners": jax.random.randint(keys[4], (2,), 0, N_DP).astype(jnp.int32),
    }


momentum_decay = 0.9
learn_rate = 0.5


def convolve(activated, kernel):
    return lax.conv_general_dilated(activated, kernel, (1, 1), ((1, 1), (1, 1)), dimension_numbers=("NHWC", "HWIO", "NHWC"), preferred_element_type=jnp.float32)


def reference(images, kernel_weights, kernel_momentum, kernel_grads, owners):
    kernels = []
    for kernel_index in range(2):
        slot = owners[kernel_index]
        velocity = momentum_decay * kernel_momentum[slot, kernel_index] + kernel_grads[slot, kernel_index].astype(jnp.float32)
        updated = kernel_weights[slot, kernel_index].astype(jnp.float32) - learn_rate * velocity
        kernels.append(updated.astype(jnp.bfloat16))
    activated = jax.nn.silu(images.astype(jnp.float32)).astype(jnp.bfloat16)
    hidden = (images.astype(jnp.float32) + convolve(activated, kernels[0])).astype(jnp.bfloat16)
    activated = jax.nn.silu(hidden.astype(jnp.float32)).astype(jnp.bfloat16)
    return (hidden.astype(jnp.float32) + convolve(activated, kernels[1])).astype(jnp.bfloat16)
```

```python
import functools

import jax
import jax.numpy as jnp
from jax import lax
from jax.experimental import pallas as pl
from jax.experimental.pallas import tpu as pltpu
from jax.sharding import PartitionSpec as P

momentum_decay = 0.9
learn_rate = 0.5
MESH = pl.DeviceIdType.MESH
fine_chunks = 15
coarse_chunks = 9
pair_hop = 3
hop = 6
slow_hop = 4


class Place:
    def __init__(self, groups, dp):
        self.groups, self.dp, self.last = groups, dp, dp // 4 - 1
        self.group, self.at = lax.axis_index("groups"), lax.axis_index("dp")
        self.z, self.y, self.core = self.at // 4, (self.at // 2) % 2, self.at % 2
        self.mate = self.at + 1 - 2 * self.core
        self.beside = self.at - 1 + 2 * self.core
        self.across = self.at + 2 - 4 * self.y
        self.share = 2 * self.group + self.core
        self.others = [lax.rem(self.group + step, groups) for step in range(1, groups)]
        self.has_beside = (self.beside >= 0) & (self.beside < dp)

    def meet(self):
        barrier = pltpu.get_barrier_semaphore()

        def greet(**where):
            pl.semaphore_signal(barrier, inc=1, device_id=where, device_id_type=MESH)

        greet(dp=self.mate)
        greet(dp=self.across)
        for other in self.others:
            greet(groups=other)
        pl.when(self.has_beside)(lambda: greet(dp=self.beside))
        pl.when(self.z > 0)(lambda: greet(dp=self.at - 4))
        pl.when(self.z < self.last)(lambda: greet(dp=self.at + 4))
        more = [
            jnp.where(there, 1, 0)
            for there in (self.has_beside, self.z > 0, self.z < self.last)
        ]
        pl.semaphore_wait(barrier, 1 + self.groups + sum(more))


def remote(src, dst, sem, k, **where):
    return pltpu.make_async_remote_copy(
        src, dst, sem.at[0, k], sem.at[1, k], device_id=where, device_id_type=MESH
    )


class Stream:
    def __init__(self, place, col, out, col_in, joined, fwd, fwd_in, back, back_in, done, sems):
        self.__dict__.update(place=place, col=col, out=out, col_in=col_in, joined=joined)
        self.__dict__.update(fwd=fwd, fwd_in=fwd_in, back=back, back_in=back_in, done=done)
        self.col_sem, self.fwd_sem, self.back_sem, self.mate_sem = sems[:4]
        self.cross_sem, self.pass_sem, self.keep_sem = sems[4:]

    def to_col(self, k):
        return remote(self.col.at[k], self.col_in.at[k], self.col_sem, k, dp=self.place.across)

    def to_fwd(self, k, up=4):
        return remote(self.fwd.at[k], self.fwd_in.at[k], self.fwd_sem, k, dp=self.place.at + up)

    def to_back(self, k, down=4):
        return remote(self.back.at[k], self.back_in.at[k], self.back_sem, k, dp=self.place.at - down)

    def keep(self, k):
        return pltpu.make_async_copy(
            self.done.at[k], self.out.at[k, self.place.share], self.keep_sem.at[k]
        )

    def to_mate(self, k):
        return remote(
            self.done.at[k], self.out.at[k, self.place.share], self.mate_sem, k, dp=self.place.mate
        )

    def to_cross(self, k, i):
        return remote(
            self.done.at[k], self.out.at[k, self.place.share], self.cross_sem.at[i], k,
            groups=self.place.others[i],
        )

    def to_pass(self, k, i):
        p = self.place
        slot = 2 * lax.rem(p.group + p.groups - 1 - i, p.groups) + p.core
        return remote(self.out.at[k, slot], self.out.at[k, slot], self.pass_sem.at[i], k, dp=p.mate)

    def join_col(self, k):
        self.to_col(k).wait_recv()
        self.joined[k] = self.col[k] + self.col_in[k]

    def go_fwd(self, k):
        p = self.place

        @pl.when(p.z == 0)
        def _():
            self.fwd[k] = self.joined[k]

        @pl.when(p.z > 0)
        def _():
            self.to_fwd(k, -4).wait_recv()
            self.fwd[k] = self.joined[k] + self.fwd_in[k]

        pl.when(p.z < p.last)(lambda: self.to_fwd(k).start())

    def go_back(self, k):
        p = self.place

        @pl.when(p.z == p.last)
        def _():
            self.back[k] = self.joined[k]

        @pl.when(p.z < p.last)
        def _():
            self.to_back(k, -4).wait_recv()
            self.back[k] = self.joined[k] + self.back_in[k]

        pl.when(p.z > 0)(lambda: self.to_back(k).start())

    def finish(self, k):
        p = self.place

        @pl.when(p.z < p.last)
        def _():
            self.done[k] = self.fwd[k] + self.back_in[k]

        @pl.when(p.z == p.last)
        def _():
            self.done[k] = self.fwd[k]

        for i in range(p.groups - 1):
            self.to_cross(k, i).start()
        self.to_mate(k).start()
        self.keep(k).start()

    def pass_on(self, k):
        for i in range(self.place.groups - 1):
            self.to_cross(k, i).wait_recv()
            self.to_pass(k, i).start()

    def steps(self, chunks, hop):
        return chunks + hop * (self.place.last + 2)

    def step(self, t, chunks, hop):
        p = self.place
        at_step(t - hop, chunks, self.join_col)
        at_step(t - hop - p.z * hop, chunks, self.go_fwd)
        at_step(t - hop - (p.last - p.z) * hop, chunks, self.go_back)
        at_step(t - hop - p.last * hop, chunks, self.finish)
        at_step(t - hop - p.last * hop - hop, chunks, self.pass_on)

    def drain(self, k):
        p = self.place
        self.to_col(k).wait_send()
        pl.when(p.z < p.last)(lambda: self.to_fwd(k).wait_send())
        pl.when(p.z > 0)(lambda: self.to_back(k).wait_send())
        self.to_mate(k).wait()
        self.keep(k).wait()
        for i in range(p.groups - 1):
            self.to_cross(k, i).wait_send()
            self.to_pass(k, i).wait()

    @staticmethod
    def scratch(chunks, part, width, groups):
        piece = pltpu.VMEM((chunks, part, width), jnp.bfloat16)
        sems = pltpu.SemaphoreType.DMA((2, chunks))
        many = pltpu.SemaphoreType.DMA((groups - 1, 2, chunks))
        return [piece] * 7 + [sems] * 4 + [many] * 2 + [pltpu.SemaphoreType.DMA((chunks,))]


def half_rows(part):
    return -(-(part // 2) // 8) * 8


def packed_rows(part, width):
    return width // 128 * part + (half_rows(part) if width % 128 else 0)


def packed(v):
    part, width = v.shape
    full, half = width // 128 * 128, half_rows(part)
    blocks = [v[:, i : i + 128] for i in range(0, full, 128)]
    if full < width:
        low, high = v[:half, full:], v[half:, full:]
        if part < 2 * half:
            high = jnp.concatenate(
                [high, jnp.zeros((2 * half - part, width - full), v.dtype)], axis=0
            )
        blocks.append(jnp.concatenate([low, high], axis=1))
    return jnp.concatenate(blocks, axis=0)


def unpack(k_ref, natural):
    chunks, shares, _, _ = k_ref.shape
    depth, width = natural.shape
    part = depth // (chunks * shares)
    full, half = width // 128 * 128, half_rows(part)
    for piece in range(chunks * shares):
        v = k_ref[piece // shares, piece % shares].astype(jnp.float32)
        base = piece * part
        for i in range(full // 128):
            natural[base : base + part, i * 128 : (i + 1) * 128] = v[i * part : (i + 1) * part]
        if full < width:
            rest = v[full // 128 * part :]
            natural[base : base + half, full:] = rest[:, : width - full]
            natural[base + half : base + part, full:] = rest[: part - half, width - full :]


def at_step(k, chunks, what):
    pl.when((k >= 0) & (k < chunks))(lambda: what(k))


def each(chunks, what):
    def body(k, carry):
        what(k)
        return carry

    lax.fori_loop(0, chunks, body, 0)


class Edges:
    def __init__(self, place, first, final, out, sem):
        self.place, self.first, self.final, self.out, self.sem = place, first, final, out, sem

    def down(self, k, to=1):
        return remote(self.final(k), self.out(0, k), self.sem.at[0], k, dp=self.place.at + to)

    def up(self, k, to=1):
        return remote(self.first(k), self.out(1, k), self.sem.at[1], k, dp=self.place.at - to)

    def start(self, k):
        at, dp = self.place.at, self.place.dp
        pl.when(at < dp - 1)(lambda: self.down(k).start())
        pl.when(at > 0)(lambda: self.up(k).start())

    def drain(self, k):
        at, dp = self.place.at, self.place.dp

        @pl.when(at < dp - 1)
        def _():
            self.down(k).wait_send()
            self.up(k, -1).wait_recv()

        @pl.when(at > 0)
        def _():
            self.up(k).wait_send()
            self.down(k, -1).wait_recv()


class Renewal:
    def __init__(self, place, mask, base, state, bufs, col, pair_out, pair_in, load_sem, pair_sem):
        self.place, self.mask, self.base = place, mask, base
        self.state, self.bufs = state, bufs
        self.col, self.pair_out, self.pair_in = col, pair_out, pair_in
        self.load_sem, self.pair_sem = load_sem, pair_sem

    def loads(self, k):
        src = pl.ds(2 * self.place.group, 2)
        return [
            pltpu.make_async_copy(ref.at[self.base + k, src], buf.at[k], self.load_sem.at[i, k])
            for i, (ref, buf) in enumerate(zip(self.state, self.bufs))
        ]

    def start(self, k):
        for copy in self.loads(k):
            copy.start()

    def to_pair(self, k):
        return remote(
            self.pair_out.at[k], self.pair_in.at[k], self.pair_sem, k, dp=self.place.mate
        )

    def renew(self, k):
        for copy in self.loads(k):
            copy.wait()
        w, m, g = self.bufs
        mine = self.mask > 0.5

        def new(c):
            velocity = momentum_decay * m[k, c] + g[k, c].astype(jnp.float32)
            updated = w[k, c].astype(jnp.float32) - learn_rate * velocity
            return packed(jnp.where(mine, updated, 0.0)).astype(jnp.bfloat16)

        self.pair_out[k] = new(1 - self.place.core)
        self.to_pair(k).start()
        self.col[k] = new(self.place.core)

    def join(self, k):
        self.to_pair(k).wait_recv()
        self.col[k] = self.col[k] + self.pair_in[k]

    @staticmethod
    def scratch(chunks, part, width):
        load = lambda dtype: pltpu.VMEM((chunks, 2, part, width), dtype)
        piece = pltpu.VMEM((chunks, packed_rows(part, width), 128), jnp.bfloat16)
        return [load(jnp.bfloat16), load(jnp.float32), load(jnp.bfloat16), piece, piece] + [
            pltpu.SemaphoreType.DMA((3, chunks)),
            pltpu.SemaphoreType.DMA((2, chunks)),
        ]


def spread_kernel(groups, dp, mask_ref, *refs):
    first_state, second_state, x_ref, out_ref, col1_ref, rims_ref = (
        refs[:3], refs[3:6], refs[6], refs[7], refs[8], refs[9],
    )
    scratch = refs[10:]
    place = Place(groups, dp)
    one = Renewal(place, mask_ref[0], 0, first_state, scratch[:3], scratch[14], *scratch[3:7])
    two = Renewal(place, mask_ref[1], coarse_chunks, second_state, scratch[7:10], col1_ref, *scratch[10:14])
    stream = Stream(place, scratch[14], out_ref, *scratch[15:22], scratch[22:29])
    height = x_ref.shape[1]
    edges = Edges(
        place, lambda k: x_ref.at[:, 0], lambda k: x_ref.at[:, height - 1],
        lambda side, k: rims_ref.at[side], scratch[29],
    )
    each(fine_chunks, one.start)
    each(coarse_chunks, two.start)
    place.meet()

    def join(k):
        one.join(k)
        stream.to_col(k).start()

    def step(t, carry):
        at_step(t, fine_chunks, one.renew)
        at_step(t - pair_hop, fine_chunks, join)
        stream.step(t - pair_hop, fine_chunks, hop)
        late = t - fine_chunks - pair_hop
        pl.when(late == 0)(lambda: edges.start(0))
        at_step(late - 1, coarse_chunks, two.renew)
        at_step(late - 1 - pair_hop, coarse_chunks, two.join)
        return carry

    ends = (pair_hop + stream.steps(fine_chunks, hop), fine_chunks + coarse_chunks + 2 * pair_hop + 1)
    lax.fori_loop(0, max(ends), step, 0)

    def drain(k):
        one.to_pair(k).wait_send()
        stream.drain(k)

    each(fine_chunks, drain)
    each(coarse_chunks, lambda k: two.to_pair(k).wait_send())
    edges.drain(0)


def spread(kernel_weights, kernel_momentum, kernel_grads, owners, x):
    groups, dp = lax.axis_size("groups"), lax.axis_size("dp")
    _, _, rows, columns, fan_in, fan_out = kernel_weights.shape
    images, _, channels, width = x.shape
    shares, depth = 2 * groups, rows * columns * fan_in
    mine = (owners == lax.axis_index("dp")).astype(jnp.float32)
    mask = jnp.broadcast_to(mine[:, None, None], (2, 1, fan_out))
    state = (kernel_weights, kernel_momentum, kernel_grads)

    def cut(chunks):
        return [a.reshape(2 * chunks, shares, -1, fan_out) for a in state]

    fine, coarse = depth // fine_chunks // shares, depth // coarse_chunks // shares
    fine_rows, coarse_rows = packed_rows(fine, fan_out), packed_rows(coarse, fan_out)
    any_space = pl.BlockSpec(memory_space=pl.ANY)
    vmem = pl.BlockSpec(memory_space=pltpu.VMEM)
    kernel, col, rims = pl.pallas_call(
        functools.partial(spread_kernel, groups, dp),
        out_shape=[
            jax.ShapeDtypeStruct((fine_chunks, shares, fine_rows, 128), jnp.bfloat16),
            jax.ShapeDtypeStruct((coarse_chunks, coarse_rows, 128), jnp.bfloat16),
            jax.ShapeDtypeStruct((2, images, channels, width), jnp.bfloat16),
        ],
        in_specs=[vmem] + [any_space] * 7,
        out_specs=[vmem, vmem, any_space],
        scratch_shapes=Renewal.scratch(fine_chunks, fine, fan_out)
        + Renewal.scratch(coarse_chunks, coarse, fan_out)
        + [pltpu.VMEM((fine_chunks, fine_rows, 128), jnp.bfloat16)]
        + Stream.scratch(fine_chunks, fine_rows, 128, groups)
        + [pltpu.SemaphoreType.DMA((2, 2, 1))],
        compiler_params=pltpu.CompilerParams(
            collective_id=0, has_side_effects=True, vmem_limit_bytes=56 << 20
        ),
    )(mask, *cut(fine_chunks), *cut(coarse_chunks), x)
    return kernel, col, rims


def silu(v):
    return v / (1.0 + jnp.exp(-v))


def conv_image(x_ref, top_ref, bottom_ref, o_ref, patch, wide, between=lambda row: None):
    height, channels, width = x_ref.shape
    at = lax.axis_index("dp")
    column = lax.broadcasted_iota(jnp.int32, (1, width), 1)

    def build(row):
        if row == 0:
            v = jnp.where(at > 0, top_ref[...].astype(jnp.float32), 0.0)
        elif row == height + 1:
            v = jnp.where(at < lax.axis_size("dp") - 1, bottom_ref[...].astype(jnp.float32), 0.0)
        else:
            v = x_ref[row - 1]
        a = silu(v.astype(jnp.float32))
        before = jnp.where(column == 0, 0.0, pltpu.roll(a, 1, 1))
        after = jnp.where(column == width - 1, 0.0, pltpu.roll(a, width - 1, 1))
        for dc, part in enumerate((before, a, after)):
            patch[row, dc * channels : (dc + 1) * channels] = part.astype(jnp.bfloat16)

    built = 0
    for row in range(0, height, 2):
        between(row)
        while built < row + 4:
            build(built)
            built += 1
        rhs = jnp.concatenate(
            [
                jnp.concatenate([patch[row + dr], patch[row + dr + 1]], axis=1)
                for dr in range(3)
            ],
            axis=0,
        )
        acc = jnp.dot(wide[...], rhs, preferred_element_type=jnp.float32)
        for i in range(2):
            x = x_ref[row + i].astype(jnp.float32)
            o_ref[row + i] = (x + acc[:, i * width : (i + 1) * width]).astype(o_ref.dtype)


def first_kernel(groups, dp, x_ref, top_ref, bottom_ref, k_ref, col_ref, o_ref, out_ref, rims_ref,
                 patch, wide, natural, borders, edge_sem, *scratch):
    place = Place(groups, dp)
    image, images = pl.program_id(0), pl.num_programs(0)
    height = x_ref.shape[1]
    stream = Stream(place, col_ref, out_ref, *scratch[:7], scratch[7:])
    edges = Edges(
        place, lambda k: borders.at[k, 0], lambda k: borders.at[k, 1],
        lambda side, k: rims_ref.at[side, k], edge_sem,
    )

    @pl.when(image == 0)
    def _():
        place.meet()
        unpack(k_ref, natural)
        wide[...] = natural[...].T.astype(jnp.bfloat16)

    def step(t, carry=0):
        at_step(t, coarse_chunks, lambda k: stream.to_col(k).start())
        stream.step(t, coarse_chunks, slow_hop)
        return carry

    def between(row):
        if row % (height // 2) == 0:
            now = 4 * image + row // (height // 2) * 2
            step(now)
            step(now + 1)

    conv_image(x_ref.at[0], top_ref.at[0, 0], bottom_ref.at[0, 0], o_ref.at[0], patch, wide, between)
    borders[image, 0] = o_ref[0, 0]
    borders[image, 1] = o_ref[0, height - 1]
    edges.start(image)

    @pl.when(image == images - 1)
    def _():
        count = borders.shape[0]
        lax.fori_loop(4 * count, max(4 * count, stream.steps(coarse_chunks, slow_hop)), step, 0)
        each(coarse_chunks, stream.drain)
        each(count, edges.drain)


def second_kernel(x_ref, top_ref, bottom_ref, k_ref, o_ref, patch, wide, natural):
    @pl.when(pl.program_id(0) == 0)
    def _():
        unpack(k_ref, natural)
        wide[...] = natural[...].T.astype(jnp.bfloat16)

    conv_image(x_ref.at[0], top_ref.at[0, 0], bottom_ref.at[0, 0], o_ref.at[0], patch, wide)


def conv_specs(x, kernel):
    images, height, channels, width = x.shape
    image = pl.BlockSpec((1, height, channels, width), lambda i: (i, 0, 0, 0))
    top = pl.BlockSpec((1, 1, channels, width), lambda i: (0, i, 0, 0))
    bottom = pl.BlockSpec((1, 1, channels, width), lambda i: (1, i, 0, 0))
    scratch = [
        pltpu.VMEM((height + 2, 3 * channels, width), jnp.bfloat16),
        pltpu.VMEM((channels, 9 * channels), jnp.bfloat16),
        pltpu.VMEM((9 * channels, channels), jnp.float32),
    ]
    whole = pl.BlockSpec(kernel.shape, lambda i: (0, 0, 0, 0))
    return image, [image, top, bottom, whole], scratch


def first_conv(x, rims, kernel, col):
    groups, dp = lax.axis_size("groups"), lax.axis_size("dp")
    images, height, channels, width = x.shape
    chunks, part, fan_out = col.shape
    image, in_specs, scratch = conv_specs(x, kernel)
    any_space = pl.BlockSpec(memory_space=pl.ANY)
    hidden, second, rims = pl.pallas_call(
        functools.partial(first_kernel, groups, dp),
        out_shape=[
            jax.ShapeDtypeStruct(x.shape, x.dtype),
            jax.ShapeDtypeStruct((chunks, 2 * groups, part, fan_out), jnp.bfloat16),
            jax.ShapeDtypeStruct(rims.shape, rims.dtype),
        ],
        grid=(images,),
        in_specs=in_specs + [pl.BlockSpec(col.shape, lambda i: (0, 0, 0))],
        out_specs=[image, any_space, any_space],
        scratch_shapes=scratch
        + [
            pltpu.VMEM((images, 2, channels, width), jnp.bfloat16),
            pltpu.SemaphoreType.DMA((2, 2, images)),
        ]
        + Stream.scratch(chunks, part, fan_out, groups),
        compiler_params=pltpu.CompilerParams(
            collective_id=1, has_side_effects=True, vmem_limit_bytes=56 << 20
        ),
    )(x, rims, rims, kernel, col)
    return hidden, second, rims


def second_conv(x, rims, kernel):
    image, in_specs, scratch = conv_specs(x, kernel)
    return pl.pallas_call(
        second_kernel,
        out_shape=jax.ShapeDtypeStruct(x.shape, x.dtype),
        grid=(x.shape[0],),
        in_specs=in_specs,
        out_specs=image,
        scratch_shapes=scratch,
        compiler_params=pltpu.CompilerParams(vmem_limit_bytes=56 << 20),
    )(x, rims, rims, kernel)


def local(images, kernel_weights, kernel_momentum, kernel_grads, owners):
    x = images.transpose(0, 1, 3, 2)
    kernel, col, rims = spread(kernel_weights, kernel_momentum, kernel_grads, owners, x)
    hidden, kernel, rims = first_conv(x, rims, kernel, col)
    return second_conv(hidden, rims, kernel).transpose(0, 1, 3, 2)


def solution(mesh):
    placed = (
        P("groups", "dp", None, None),
        P("dp", None, None, None, None, None),
        P("dp", None, None, None, None, None),
        P("dp", None, None, None, None, None),
        P(),
    )
    return jax.shard_map(
        local, mesh=mesh, in_specs=placed, out_specs=P("groups", "dp", None, None), check_vma=False
    )
```

```python
import functools

import jax
import jax.numpy as jnp
from jax import lax
from jax.experimental import pallas as pl
from jax.experimental.pallas import tpu as pltpu
from jax.sharding import PartitionSpec as P

momentum_decay = 0.9
learn_rate = 0.5
MESH = pl.DeviceIdType.MESH
fine_chunks = 15
coarse_chunks = 5
pair_hop = 3
fine_hop = 5
coarse_hop = 2
coarse_stride = 3
edge_start = 18
edge_stride = 3
build_back = 8
near, far = 0.75, 1.5
log2_e = 1.4426950408889634


class Place:
    def __init__(self, groups, dp):
        self.groups, self.dp, self.last = groups, dp, dp // 4 - 1
        self.group, self.at = lax.axis_index("groups"), lax.axis_index("dp")
        self.z, self.y, self.core = self.at // 4, (self.at // 2) % 2, self.at % 2
        self.mate = self.at + 1 - 2 * self.core
        self.beside = self.at - 1 + 2 * self.core
        self.across = self.at + 2 - 4 * self.y
        self.share = 2 * self.group + self.core
        self.others = [lax.rem(self.group + step, groups) for step in range(1, groups)]
        self.has_beside = (self.beside >= 0) & (self.beside < dp)

    def meet(self):
        barrier = pltpu.get_barrier_semaphore()

        def greet(**where):
            pl.semaphore_signal(barrier, inc=1, device_id=where, device_id_type=MESH)

        greet(dp=self.mate)
        greet(dp=self.across)
        for other in self.others:
            greet(groups=other)
        pl.when(self.has_beside)(lambda: greet(dp=self.beside))
        pl.when(self.z > 0)(lambda: greet(dp=self.at - 4))
        pl.when(self.z < self.last)(lambda: greet(dp=self.at + 4))
        more = [
            jnp.where(there, 1, 0)
            for there in (self.has_beside, self.z > 0, self.z < self.last)
        ]
        pl.semaphore_wait(barrier, 1 + self.groups + sum(more))


def remote(src, dst, sem, k, **where):
    return pltpu.make_async_remote_copy(
        src, dst, sem.at[0, k], sem.at[1, k], device_id=where, device_id_type=MESH
    )


def at_step(k, chunks, what):
    pl.when((k >= 0) & (k < chunks))(lambda: what(k))


def at_stride(k, stride, chunks, what):
    pl.when((k >= 0) & (k % stride == 0) & (k < chunks * stride))(lambda: what(k // stride))


def each(chunks, what):
    def body(k, carry):
        what(k)
        return carry

    lax.fori_loop(0, chunks, body, 0)


def half_rows(part):
    return -(-(part // 2) // 8) * 8


def packed_rows(part, width):
    return width // 128 * part + (half_rows(part) if width % 128 else 0)


def packed(v):
    part, width = v.shape
    full, half = width // 128 * 128, half_rows(part)
    blocks = [v[:, i : i + 128] for i in range(0, full, 128)]
    if full < width:
        low, high = v[:half, full:], v[half:, full:]
        if part < 2 * half:
            high = jnp.concatenate(
                [high, jnp.zeros((2 * half - part, width - full), v.dtype)], axis=0
            )
        blocks.append(jnp.concatenate([low, high], axis=1))
    return jnp.concatenate(blocks, axis=0)


def unpack(k_ref, natural, k):
    _, shares, _, _ = k_ref.shape
    taps, depth, width = natural.shape
    depth = width * taps
    unit = depth // (k_ref.shape[0] * shares)
    part = taps * unit
    full, half = width // 128 * 128, half_rows(part)
    for share in range(shares):
        v = k_ref[k, share].astype(jnp.float32)
        base = (k * shares + share) * unit

        def put(low, high, lane, piece):
            for row in range(low, high, 8):
                at = pl.ds(pl.multiple_of(base + row % unit, 8), 8)
                lanes = slice(lane, lane + piece.shape[1])
                natural[row // unit, at, lanes] = piece[row - low : row - low + 8]

        for i in range(full // 128):
            put(0, part, i * 128, v[i * part : (i + 1) * part])
        if full < width:
            rest = v[full // 128 * part :]
            put(0, half, full, rest[:, : width - full])
            put(half, part, full, rest[: part - half, width - full :])


class Stream:
    def __init__(self, place, chunks, lead, hop, land, col, out, bufs, sems):
        self.place, self.chunks, self.lead, self.hop, self.land = place, chunks, lead, hop, land
        self.col, self.out = col, out
        self.col_in, self.joined, self.fwd, self.fwd_in, self.back, self.back_in = bufs
        self.col_sem, self.fwd_sem, self.back_sem, self.mate_sem = sems[:4]
        self.cross_sem, self.pass_sem = sems[4:]

    def to_col(self, k):
        return remote(self.col.at[k], self.col_in.at[k], self.col_sem, k, dp=self.place.across)

    def to_fwd(self, k, up=4):
        return remote(self.fwd.at[k], self.fwd_in.at[k], self.fwd_sem, k, dp=self.place.at + up)

    def to_back(self, k, down=4):
        return remote(self.back.at[k], self.back_in.at[k], self.back_sem, k, dp=self.place.at - down)

    def to_mate(self, k):
        done = self.out.at[k, self.place.share]
        return remote(done, done, self.mate_sem, k, dp=self.place.mate)

    def to_cross(self, k, i):
        done = self.out.at[k, self.place.share]
        return remote(done, done, self.cross_sem.at[i], k, groups=self.place.others[i])

    def to_pass(self, k, i):
        p = self.place
        slot = 2 * lax.rem(p.group + p.groups - 1 - i, p.groups) + p.core
        done = self.out.at[k, slot]
        return remote(done, done, self.pass_sem.at[i], k, dp=p.mate)

    def join_col(self, k):
        self.to_col(k).wait_recv()
        self.joined[k] = self.col[k] + self.col_in[k]

    def go_fwd(self, k):
        p = self.place

        @pl.when(p.z == 0)
        def _():
            self.fwd[k] = self.joined[k]

        @pl.when(p.z > 0)
        def _():
            self.to_fwd(k, -4).wait_recv()
            self.fwd[k] = self.joined[k] + self.fwd_in[k]

        pl.when(p.z < p.last)(lambda: self.to_fwd(k).start())

    def go_back(self, k):
        p = self.place

        @pl.when(p.z == p.last)
        def _():
            self.back[k] = self.joined[k]

        @pl.when(p.z < p.last)
        def _():
            self.to_back(k, -4).wait_recv()
            self.back[k] = self.joined[k] + self.back_in[k]

        pl.when(p.z > 0)(lambda: self.to_back(k).start())

    def finish(self, k):
        p = self.place

        @pl.when(p.z < p.last)
        def _():
            self.out[k, p.share] = self.fwd[k] + self.back_in[k]

        @pl.when(p.z == p.last)
        def _():
            self.out[k, p.share] = self.fwd[k]

        for i in range(p.groups - 1):
            self.to_cross(k, i).start()
        self.to_mate(k).start()

    def pass_on(self, k):
        for i in range(self.place.groups - 1):
            self.to_cross(k, i).wait_recv()
            self.to_pass(k, i).start()

    def arrive(self, k):
        self.to_mate(k).wait_recv()
        for i in range(self.place.groups - 1):
            self.to_pass(k, i).wait_recv()
        self.land(k)

    @staticmethod
    def steps(chunks, lead, hop, last):
        return chunks + lead + (last + 1) * hop + 1

    def step(self, t):
        p, chunks, hop = self.place, self.chunks, self.hop
        t = t - self.lead
        at_step(t, chunks, self.join_col)
        at_step(t - p.z * hop, chunks, self.go_fwd)
        at_step(t - (p.last - p.z) * hop, chunks, self.go_back)
        at_step(t - p.last * hop, chunks, self.finish)
        at_step(t - p.last * hop - hop, chunks, self.pass_on)
        at_step(t - p.last * hop - hop - 1, chunks, self.arrive)

    def drain(self, k):
        p = self.place
        self.to_col(k).wait_send()
        pl.when(p.z < p.last)(lambda: self.to_fwd(k).wait_send())
        pl.when(p.z > 0)(lambda: self.to_back(k).wait_send())
        self.to_mate(k).wait_send()
        for i in range(p.groups - 1):
            self.to_cross(k, i).wait_send()
            self.to_pass(k, i).wait_send()

    @staticmethod
    def scratch(chunks, part, width, groups):
        piece = pltpu.VMEM((chunks, packed_rows(part, width), 128), jnp.bfloat16)
        out = pltpu.VMEM((chunks, 2 * groups, packed_rows(part, width), 128), jnp.bfloat16)
        sems = pltpu.SemaphoreType.DMA((2, chunks))
        many = pltpu.SemaphoreType.DMA((groups - 1, 2, chunks))
        return [piece, out] + [piece] * 6 + [sems] * 4 + [many] * 2


class Edges:
    def __init__(self, place, first, final, out, sem):
        self.place, self.first, self.final, self.out, self.sem = place, first, final, out, sem

    def down(self, k, to=1):
        return remote(self.final(k), self.out(0, k), self.sem.at[0], k, dp=self.place.at + to)

    def up(self, k, to=1):
        return remote(self.first(k), self.out(1, k), self.sem.at[1], k, dp=self.place.at - to)

    def start(self, k):
        at, dp = self.place.at, self.place.dp
        pl.when(at < dp - 1)(lambda: self.down(k).start())
        pl.when(at > 0)(lambda: self.up(k).start())

    def drain(self, k):
        at, dp = self.place.at, self.place.dp

        @pl.when(at < dp - 1)
        def _():
            self.down(k).wait_send()
            self.up(k, -1).wait_recv()

        @pl.when(at > 0)
        def _():
            self.up(k).wait_send()
            self.down(k, -1).wait_recv()


class Renewal:
    def __init__(self, place, mine, which, state, col, scratch):
        self.place, self.mine, self.which, self.state, self.col = place, mine, which, state, col
        self.bufs = scratch[:3]
        self.pair_out, self.pair_in, self.load_sem, self.pair_sem = scratch[3:]

    def loads(self, k):
        src = pl.ds(2 * self.place.group, 2)
        return [
            pltpu.make_async_copy(
                ref.at[self.which, :, k, src], buf.at[k], self.load_sem.at[i, k]
            )
            for i, (ref, buf) in enumerate(zip(self.state, self.bufs))
        ]

    def start(self, k):
        for copy in self.loads(k):
            copy.start()

    def to_pair(self, k):
        return remote(
            self.pair_out.at[k], self.pair_in.at[k], self.pair_sem, k, dp=self.place.mate
        )

    def renew(self, k):
        for copy in self.loads(k):
            copy.wait()
        w, m, g = self.bufs

        def new(c):
            velocity = momentum_decay * m[k, :, c] + g[k, :, c].astype(jnp.float32)
            updated = w[k, :, c].astype(jnp.float32) - learn_rate * velocity
            updated = updated.reshape(-1, updated.shape[-1])
            return packed(jnp.where(self.mine, updated, 0.0)).astype(jnp.bfloat16)

        self.pair_out[k] = new(1 - self.place.core)
        self.to_pair(k).start()
        self.col[k] = new(self.place.core)

    def join(self, k):
        self.to_pair(k).wait_recv()
        self.col[k] = self.col[k] + self.pair_in[k]

    @staticmethod
    def scratch(chunks, taps, unit, width):
        load = lambda dtype: pltpu.VMEM((chunks, taps, 2, unit, width), dtype)
        piece = pltpu.VMEM((chunks, packed_rows(taps * unit, width), 128), jnp.bfloat16)
        return [load(jnp.bfloat16), load(jnp.float32), load(jnp.bfloat16), piece, piece] + [
            pltpu.SemaphoreType.DMA((3, chunks)),
            pltpu.SemaphoreType.DMA((2, chunks)),
        ]


def silu(v):
    return v / (1.0 + jnp.exp2(v * -log2_e))


def spread_rows(d):
    a, b = near * near, far * far
    even_near, odd_near = d[4] - b * d[2], near * (d[3] - b * d[1])
    even_far, odd_far = d[4] - a * d[2], far * (d[3] - a * d[1])
    return (
        d[4] + (a * b) * d[0] - (a + b) * d[2],
        even_near + odd_near,
        even_near - odd_near,
        even_far + odd_far,
        even_far - odd_far,
        d[5] + (a * b) * d[1] - (a + b) * d[3],
    )


def spread_taps(k):
    a, b = near * near, far * far
    n, f = 1.0 / (2.0 * a * (a - b)), 1.0 / (2.0 * b * (b - a))
    even_near, odd_near = n * k[0] + (n * a) * k[2], (n * near) * k[1]
    even_far, odd_far = f * k[0] + (f * b) * k[2], (f * far) * k[1]
    return (
        (1.0 / (a * b)) * k[0],
        even_near + odd_near,
        even_near - odd_near,
        even_far + odd_far,
        even_far - odd_far,
        k[2],
    )


def gather_rows(m):
    a, b = near * near, far * far
    even_near, odd_near = m[1] + m[2], m[1] - m[2]
    even_far, odd_far = m[3] + m[4], m[3] - m[4]
    return (
        m[0] + even_near + even_far,
        near * odd_near + far * odd_far,
        a * even_near + b * even_far,
        (a * near) * odd_near + (b * far) * odd_far + m[5],
    )


parts, rows_out, rows_in = 6, 4, 6


def transform(natural, wide, block):
    taps, _, width = natural.shape
    cols = pl.ds(pl.multiple_of(block * 128, 128), 128)
    for out in range(0, width, 128):
        end = min(out + 128, width)
        k = [natural[tap, cols, out:end].T for tap in range(taps)]
        for j, part in enumerate(spread_taps(k)):
            wide[j, out:end, cols] = part.astype(jnp.bfloat16)


def block_kernel(groups, dp, owners_ref, *refs):
    fine_state, coarse_state, x_ref, y_ref = refs[:3], refs[3:6], refs[6], refs[7]
    scratch = list(refs[8:])

    def take(count):
        taken = scratch[:count]
        del scratch[:count]
        return taken

    act, rims, natural, wide, patch_0, patch_1, acc_0, acc_1 = take(8)
    x_sem, y_sem, x_edge_sem, hidden_edge_sem = take(4)
    one_scratch, two_scratch = take(7), take(7)
    first_scratch, second_scratch = take(14), take(14)

    place = Place(groups, dp)
    at, last = place.at, place.last
    _, images, height, channels, width = act.shape
    units = 2 * images
    taps = natural.shape[0]
    depth = taps * channels
    blocks = -(-depth // 128)
    per_block = 128 * fine_chunks // depth

    def mine(which):
        flag = jnp.where(owners_ref[which] == at, 1.0, 0.0)
        return jnp.full((1, channels), flag, jnp.float32) > 0.5

    def land_first(k):
        unpack(first.out, natural, k)

        @pl.when((k % per_block == per_block - 1) | (k == fine_chunks - 1))
        def _():
            transform(natural, wide, k // per_block)

    def land_second(k):
        unpack(second.out, natural, k)

    first = Stream(
        place, fine_chunks, fine_hop, fine_hop, land_first,
        first_scratch[0], first_scratch[1], first_scratch[2:8], first_scratch[8:],
    )
    second = Stream(
        place, coarse_chunks, coarse_hop, coarse_hop, land_second,
        second_scratch[0], second_scratch[1], second_scratch[2:8], second_scratch[8:],
    )
    one = Renewal(place, mine(0), 0, fine_state, first.col, one_scratch)
    two = Renewal(place, mine(1), 1, coarse_state, second.col, two_scratch)
    x_edges = Edges(
        place, lambda k: x_ref.at[k, 0], lambda k: x_ref.at[k, height - 1],
        lambda side, k: rims.at[0, side, k], x_edge_sem,
    )
    hidden_edges = Edges(
        place, lambda k: act.at[1, k, 0], lambda k: act.at[1, k, height - 1],
        lambda side, k: rims.at[1, side, k], hidden_edge_sem,
    )

    def x_load(k):
        return pltpu.make_async_copy(x_ref.at[k], act.at[0, k], x_sem.at[k])

    def y_store(k):
        return pltpu.make_async_copy(act.at[0, k], y_ref.at[k], y_sem.at[k])

    column = lax.broadcasted_iota(jnp.int32, (16, width), 1)
    not_first = jnp.where(column == 0, 0.0, 1.0).astype(jnp.bfloat16)
    not_last = jnp.where(column == width - 1, 0.0, 1.0).astype(jnp.bfloat16)

    def build(n, patch, e):
        layer, image = n // images, n % images
        lanes = pl.ds(e, 16)
        a = []
        for row in range(-1, height + 1):
            if row < 0:
                v = jnp.where(at > 0, rims[layer, 0, image, lanes].astype(jnp.float32), 0.0)
            elif row == height:
                v = jnp.where(at < dp - 1, rims[layer, 1, image, lanes].astype(jnp.float32), 0.0)
            else:
                v = act[layer, image, row, lanes].astype(jnp.float32)
            a.append(silu(v))
        for q in range(height // rows_out):
            d = a[q * rows_out : q * rows_out + rows_in]
            for j, v in enumerate(spread_rows(d)):
                v = v.astype(jnp.bfloat16)
                before = pltpu.roll(v, 1, 1) * not_first
                after = pltpu.roll(v, width - 1, 1) * not_last
                for tap, part in enumerate((before, v, after)):
                    patch[j, pl.ds(tap * channels + e, 16), q * width : (q + 1) * width] = part

    def settle(n, acc, e):
        layer, image = n // images, n % images
        lanes = pl.ds(e, 16)
        for r, v in enumerate(gather_rows([acc[j, lanes] for j in range(parts)])):
            for q in range(height // rows_out):
                row = q * rows_out + r
                x = act[layer, image, row, lanes].astype(jnp.float32)
                act[1 - layer, image, row, lanes] = (
                    x + v[:, q * width : (q + 1) * width]
                ).astype(jnp.bfloat16)

    slabs = list(range(0, channels, 16))

    def work(n, patch, patch_next, acc, acc_before):
        after, before = jnp.minimum(n + 1, units - 1), jnp.maximum(n - 1, 0)
        for j in range(parts):
            acc[j] = jnp.dot(
                wide[j, :, :depth], patch[j], preferred_element_type=jnp.float32
            )
            for e in slabs[len(slabs) * j // parts : len(slabs) * (j + 1) // parts]:
                build(after, patch_next, e)
                settle(before, acc_before, e)

    fine_steps = pair_hop + Stream.steps(fine_chunks, fine_hop, fine_hop, last)
    coarse_steps = 1 + Stream.steps(coarse_chunks, coarse_hop, coarse_hop, last)
    early = max(coarse_steps - images, 0)
    total = max(fine_steps, early * coarse_stride, edge_start + edge_stride * images)
    coarse_start = total - early * coarse_stride

    each(fine_chunks, one.start)
    each(images, lambda k: x_load(k).start())
    each(coarse_chunks, two.start)
    place.meet()

    def coarse_step(q):
        at_step(q, coarse_chunks, two.renew)

        def join(k):
            two.join(k)
            second.to_col(k).start()

        at_step(q - 1, coarse_chunks, join)
        second.step(q - 1)

    def join_one(k):
        one.join(k)
        first.to_col(k).start()

    def step(t, carry):
        at_step(t, fine_chunks, one.renew)
        at_step(t - pair_hop, fine_chunks, join_one)
        first.step(t - pair_hop)
        at_stride(t - edge_start, edge_stride, images, x_edges.start)
        at_stride(t - coarse_start, coarse_stride, early, coarse_step)

        @pl.when(t == total - build_back)
        def _():
            x_load(0).wait()
            x_edges.drain(0)
            for e in slabs:
                build(0, patch_0, e)

        return carry

    lax.fori_loop(0, total, step, 0)

    def between(n):
        pl.when(n < images)(lambda: coarse_step(early + n))

        @pl.when(n == images)
        def _():
            each(blocks, lambda b: transform(natural, wide, b))

        @pl.when(n + 1 < images)
        def _():
            x_load(n + 1).wait()
            x_edges.drain(n + 1)

        at_step(n + 1 - images, images, hidden_edges.drain)
        at_step(n - 2, images, hidden_edges.start)
        at_step(n - 2 - images, images, lambda k: y_store(k).start())

    def both(t, carry):
        between(2 * t)
        work(2 * t, patch_0, patch_1, acc_0, acc_1)
        between(2 * t + 1)
        work(2 * t + 1, patch_1, patch_0, acc_1, acc_0)
        return carry

    lax.fori_loop(0, images, both, 0)
    y_store(images - 2).start()
    for e in slabs:
        settle(units - 1, acc_1, e)
    y_store(images - 1).start()

    def drain_first(k):
        one.to_pair(k).wait_send()
        first.drain(k)

    def drain_second(k):
        two.to_pair(k).wait_send()
        second.drain(k)

    each(fine_chunks, drain_first)
    each(coarse_chunks, drain_second)
    each(images, lambda k: y_store(k).wait())


def local(images, kernel_weights, kernel_momentum, kernel_grads, owners):
    groups, dp = lax.axis_size("groups"), lax.axis_size("dp")
    x = images.transpose(0, 1, 3, 2)
    _, _, taps, columns, fan_in, fan_out = kernel_weights.shape
    count, height, channels, width = x.shape
    shares, depth = 2 * groups, columns * fan_in
    padded = -(-depth // 128) * 128
    state = (kernel_weights, kernel_momentum, kernel_grads)

    def cut(chunks):
        return [a.reshape(2, taps, chunks, shares, -1, fan_out) for a in state]

    fine, coarse = depth // fine_chunks // shares, depth // coarse_chunks // shares
    any_space = pl.BlockSpec(memory_space=pl.ANY)
    smem = pl.BlockSpec(memory_space=pltpu.SMEM)
    patch = pltpu.VMEM((parts, depth, height // rows_out * width), jnp.bfloat16)
    acc = pltpu.VMEM((parts, channels, height // rows_out * width), jnp.float32)
    y = pl.pallas_call(
        functools.partial(block_kernel, groups, dp),
        out_shape=jax.ShapeDtypeStruct(x.shape, x.dtype),
        in_specs=[smem] + [any_space] * 7,
        out_specs=any_space,
        scratch_shapes=[
            pltpu.VMEM((2,) + x.shape, x.dtype),
            pltpu.VMEM((2, 2, count, channels, width), x.dtype),
            pltpu.VMEM((taps, padded, fan_out), jnp.float32),
            pltpu.VMEM((parts, fan_out, padded), jnp.bfloat16),
            patch, patch, acc, acc,
            pltpu.SemaphoreType.DMA((count,)),
            pltpu.SemaphoreType.DMA((count,)),
            pltpu.SemaphoreType.DMA((2, 2, count)),
            pltpu.SemaphoreType.DMA((2, 2, count)),
        ]
        + Renewal.scratch(fine_chunks, taps, fine, fan_out)
        + Renewal.scratch(coarse_chunks, taps, coarse, fan_out)
        + Stream.scratch(fine_chunks, taps * fine, fan_out, groups)
        + Stream.scratch(coarse_chunks, taps * coarse, fan_out, groups),
        compiler_params=pltpu.CompilerParams(
            collective_id=0, has_side_effects=True, vmem_limit_bytes=60 << 20
        ),
    )(owners, *cut(fine_chunks), *cut(coarse_chunks), x)
    return y.transpose(0, 1, 3, 2)


def solution(mesh):
    placed = (
        P("groups", "dp", None, None),
        P("dp", None, None, None, None, None),
        P("dp", None, None, None, None, None),
        P("dp", None, None, None, None, None),
        P(),
    )
    return jax.shard_map(
        local, mesh=mesh, in_specs=placed, out_specs=P("groups", "dp", None, None), check_vma=False
    )
```

```python
import functools

import jax
import jax.numpy as jnp
from jax import lax
from jax.experimental import pallas as pl
from jax.experimental.pallas import tpu as pltpu
from jax.sharding import PartitionSpec as P

momentum_decay = 0.9
learn_rate = 0.5
MESH = pl.DeviceIdType.MESH
fine_chunks = 15
coarse_chunks = 5
pair_hop = 3
fine_hop = 5
coarse_hop = 2
coarse_lead = 4
coarse_stride = 3
coarse_rate = 1
edge_start = 18
edge_stride = 3
build_back = 8
log2_e = 1.4426950408889634


class Place:
    def __init__(self, groups, dp):
        self.groups, self.dp, self.last = groups, dp, dp // 4 - 1
        self.group, self.at = lax.axis_index("groups"), lax.axis_index("dp")
        self.z, self.y, self.core = self.at // 4, (self.at // 2) % 2, self.at % 2
        self.mate = self.at + 1 - 2 * self.core
        self.beside = self.at - 1 + 2 * self.core
        self.across = self.at + 2 - 4 * self.y
        self.share = 2 * self.group + self.core
        self.others = [lax.rem(self.group + step, groups) for step in range(1, groups)]
        self.has_beside = (self.beside >= 0) & (self.beside < dp)

    def meet(self):
        barrier = pltpu.get_barrier_semaphore()

        def greet(**where):
            pl.semaphore_signal(barrier, inc=1, device_id=where, device_id_type=MESH)

        greet(dp=self.mate)
        greet(dp=self.across)
        for other in self.others:
            greet(groups=other)
        pl.when(self.has_beside)(lambda: greet(dp=self.beside))
        pl.when(self.z > 0)(lambda: greet(dp=self.at - 4))
        pl.when(self.z < self.last)(lambda: greet(dp=self.at + 4))
        more = [
            jnp.where(there, 1, 0)
            for there in (self.has_beside, self.z > 0, self.z < self.last)
        ]
        pl.semaphore_wait(barrier, 1 + self.groups + sum(more))


def remote(src, dst, sem, k, **where):
    return pltpu.make_async_remote_copy(
        src, dst, sem.at[0, k], sem.at[1, k], device_id=where, device_id_type=MESH
    )


def at_step(k, chunks, what):
    pl.when((k >= 0) & (k < chunks))(lambda: what(k))


def at_stride(k, stride, chunks, what):
    pl.when((k >= 0) & (k % stride == 0) & (k < chunks * stride))(lambda: what(k // stride))


def each(chunks, what):
    def body(k, carry):
        what(k)
        return carry

    lax.fori_loop(0, chunks, body, 0)


def half_rows(part):
    return -(-(part // 2) // 8) * 8


def packed_rows(part, width):
    return width // 128 * part + (half_rows(part) if width % 128 else 0)


def packed(v):
    part, width = v.shape
    full, half = width // 128 * 128, half_rows(part)
    blocks = [v[:, i : i + 128] for i in range(0, full, 128)]
    if full < width:
        low, high = v[:half, full:], v[half:, full:]
        if part < 2 * half:
            high = jnp.concatenate(
                [high, jnp.zeros((2 * half - part, width - full), v.dtype)], axis=0
            )
        blocks.append(jnp.concatenate([low, high], axis=1))
    return jnp.concatenate(blocks, axis=0)


def unpack(k_ref, natural, k):
    _, shares, _, _ = k_ref.shape
    taps, depth, width = natural.shape
    depth = width * taps
    unit = depth // (k_ref.shape[0] * shares)
    part = taps * unit
    full, half = width // 128 * 128, half_rows(part)
    for share in range(shares):
        v = k_ref[k, share].astype(jnp.float32)
        base = (k * shares + share) * unit

        def put(low, high, lane, piece):
            for row in range(low, high, 8):
                at = pl.ds(pl.multiple_of(base + row % unit, 8), 8)
                lanes = slice(lane, lane + piece.shape[1])
                natural[row // unit, at, lanes] = piece[row - low : row - low + 8]

        for i in range(full // 128):
            put(0, part, i * 128, v[i * part : (i + 1) * part])
        if full < width:
            rest = v[full // 128 * part :]
            put(0, half, full, rest[:, : width - full])
            put(half, part, full, rest[: part - half, width - full :])


class Stream:
    def __init__(self, place, chunks, lead, hop, land, col, out, bufs, sems):
        self.place, self.chunks, self.lead, self.hop, self.land = place, chunks, lead, hop, land
        self.col, self.out = col, out
        self.col_in, self.joined, self.fwd, self.fwd_in, self.back, self.back_in = bufs
        self.col_sem, self.fwd_sem, self.back_sem, self.mate_sem = sems[:4]
        self.cross_sem, self.pass_sem = sems[4:]

    def to_col(self, k):
        return remote(self.col.at[k], self.col_in.at[k], self.col_sem, k, dp=self.place.across)

    def to_fwd(self, k, up=4):
        return remote(self.fwd.at[k], self.fwd_in.at[k], self.fwd_sem, k, dp=self.place.at + up)

    def to_back(self, k, down=4):
        return remote(self.back.at[k], self.back_in.at[k], self.back_sem, k, dp=self.place.at - down)

    def to_mate(self, k):
        done = self.out.at[k, self.place.share]
        return remote(done, done, self.mate_sem, k, dp=self.place.mate)

    def to_cross(self, k, i):
        done = self.out.at[k, self.place.share]
        return remote(done, done, self.cross_sem.at[i], k, groups=self.place.others[i])

    def to_pass(self, k, i):
        p = self.place
        slot = 2 * lax.rem(p.group + p.groups - 1 - i, p.groups) + p.core
        done = self.out.at[k, slot]
        return remote(done, done, self.pass_sem.at[i], k, dp=p.mate)

    def join_col(self, k):
        self.to_col(k).wait_recv()
        self.joined[k] = self.col[k] + self.col_in[k]

    def go_fwd(self, k):
        p = self.place

        @pl.when(p.z == 0)
        def _():
            self.fwd[k] = self.joined[k]

        @pl.when(p.z > 0)
        def _():
            self.to_fwd(k, -4).wait_recv()
            self.fwd[k] = self.joined[k] + self.fwd_in[k]

        pl.when(p.z < p.last)(lambda: self.to_fwd(k).start())

    def go_back(self, k):
        p = self.place

        @pl.when(p.z == p.last)
        def _():
            self.back[k] = self.joined[k]

        @pl.when(p.z < p.last)
        def _():
            self.to_back(k, -4).wait_recv()
            self.back[k] = self.joined[k] + self.back_in[k]

        pl.when(p.z > 0)(lambda: self.to_back(k).start())

    def finish(self, k):
        p = self.place

        @pl.when(p.z < p.last)
        def _():
            self.out[k, p.share] = self.fwd[k] + self.back_in[k]

        @pl.when(p.z == p.last)
        def _():
            self.out[k, p.share] = self.fwd[k]

        for i in range(p.groups - 1):
            self.to_cross(k, i).start()
        self.to_mate(k).start()

    def pass_on(self, k):
        for i in range(self.place.groups - 1):
            self.to_cross(k, i).wait_recv()
            self.to_pass(k, i).start()

    def arrive(self, k):
        self.to_mate(k).wait_recv()
        for i in range(self.place.groups - 1):
            self.to_pass(k, i).wait_recv()
        self.land(k)

    @staticmethod
    def steps(chunks, lead, hop, last):
        return chunks + lead + (last + 1) * hop + 1

    def step(self, t):
        p, chunks, hop = self.place, self.chunks, self.hop
        t = t - self.lead
        at_step(t, chunks, self.join_col)
        at_step(t - p.z * hop, chunks, self.go_fwd)
        at_step(t - (p.last - p.z) * hop, chunks, self.go_back)
        at_step(t - p.last * hop, chunks, self.finish)
        at_step(t - p.last * hop - hop, chunks, self.pass_on)
        at_step(t - p.last * hop - hop - 1, chunks, self.arrive)

    def drain(self, k):
        p = self.place
        self.to_col(k).wait_send()
        pl.when(p.z < p.last)(lambda: self.to_fwd(k).wait_send())
        pl.when(p.z > 0)(lambda: self.to_back(k).wait_send())
        self.to_mate(k).wait_send()
        for i in range(p.groups - 1):
            self.to_cross(k, i).wait_send()
            self.to_pass(k, i).wait_send()

    @staticmethod
    def scratch(chunks, part, width, groups):
        piece = pltpu.VMEM((chunks, packed_rows(part, width), 128), jnp.bfloat16)
        out = pltpu.VMEM((chunks, 2 * groups, packed_rows(part, width), 128), jnp.bfloat16)
        sems = pltpu.SemaphoreType.DMA((2, chunks))
        many = pltpu.SemaphoreType.DMA((groups - 1, 2, chunks))
        return [piece, out] + [piece] * 6 + [sems] * 4 + [many] * 2


class Edges:
    def __init__(self, place, first, final, out, sem):
        self.place, self.first, self.final, self.out, self.sem = place, first, final, out, sem

    def down(self, k, to=1):
        return remote(self.final(k), self.out(0, k), self.sem.at[0], k, dp=self.place.at + to)

    def up(self, k, to=1):
        return remote(self.first(k), self.out(1, k), self.sem.at[1], k, dp=self.place.at - to)

    def start(self, k):
        at, dp = self.place.at, self.place.dp
        pl.when(at < dp - 1)(lambda: self.down(k).start())
        pl.when(at > 0)(lambda: self.up(k).start())

    def drain(self, k):
        at, dp = self.place.at, self.place.dp

        @pl.when(at < dp - 1)
        def _():
            self.down(k).wait_send()
            self.up(k, -1).wait_recv()

        @pl.when(at > 0)
        def _():
            self.up(k).wait_send()
            self.down(k, -1).wait_recv()


class Renewal:
    def __init__(self, place, mine, which, state, col, scratch):
        self.place, self.mine, self.which, self.state, self.col = place, mine, which, state, col
        self.bufs = scratch[:3]
        self.pair_out, self.pair_in, self.load_sem, self.pair_sem = scratch[3:]

    def loads(self, k):
        src = pl.ds(2 * self.place.group, 2)
        return [
            pltpu.make_async_copy(
                ref.at[self.which, :, k, src], buf.at[k], self.load_sem.at[i, k]
            )
            for i, (ref, buf) in enumerate(zip(self.state, self.bufs))
        ]

    def start(self, k):
        for copy in self.loads(k):
            copy.start()

    def to_pair(self, k):
        return remote(
            self.pair_out.at[k], self.pair_in.at[k], self.pair_sem, k, dp=self.place.mate
        )

    def renew(self, k):
        for copy in self.loads(k):
            copy.wait()
        w, m, g = self.bufs

        def new(c):
            velocity = momentum_decay * m[k, :, c] + g[k, :, c].astype(jnp.float32)
            updated = w[k, :, c].astype(jnp.float32) - learn_rate * velocity
            updated = updated.reshape(-1, updated.shape[-1])
            return packed(jnp.where(self.mine, updated, 0.0)).astype(jnp.bfloat16)

        self.pair_out[k] = new(1 - self.place.core)
        self.to_pair(k).start()
        self.col[k] = new(self.place.core)

    def join(self, k):
        self.to_pair(k).wait_recv()
        self.col[k] = self.col[k] + self.pair_in[k]

    @staticmethod
    def scratch(chunks, taps, unit, width):
        load = lambda dtype: pltpu.VMEM((chunks, taps, 2, unit, width), dtype)
        piece = pltpu.VMEM((chunks, packed_rows(taps * unit, width), 128), jnp.bfloat16)
        return [load(jnp.bfloat16), load(jnp.float32), load(jnp.bfloat16), piece, piece] + [
            pltpu.SemaphoreType.DMA((3, chunks)),
            pltpu.SemaphoreType.DMA((2, chunks)),
        ]


def silu(v):
    return v / (1.0 + jnp.exp2(v * -log2_e))


def spread_rows(d):
    return d[0] - d[2], d[1] + d[2], d[2] - d[1], d[1] - d[3]


def spread_taps(k):
    outer, inner = 0.5 * (k[0] + k[2]), 0.5 * k[1]
    return k[0], outer + inner, outer - inner, k[2]


def gather_rows(m):
    return m[0] + m[1] + m[2], m[1] - m[2] - m[3]


parts, rows_out, rows_in = 4, 2, 4


def transform(natural, wide, block):
    taps, _, width = natural.shape
    cols = pl.ds(pl.multiple_of(block * 128, 128), 128)
    for out in range(0, width, 128):
        end = min(out + 128, width)
        k = [natural[tap, cols, out:end].T for tap in range(taps)]
        for j, part in enumerate(spread_taps(k)):
            wide[j, out:end, cols] = part.astype(jnp.bfloat16)


def block_kernel(groups, dp, owners_ref, *refs):
    fine_state, coarse_state, x_ref, y_ref = refs[:3], refs[3:6], refs[6], refs[7]
    scratch = list(refs[8:])

    def take(count):
        taken = scratch[:count]
        del scratch[:count]
        return taken

    act, rims, natural, wide, patch_0, patch_1, acc_0, acc_1 = take(8)
    x_sem, y_sem, x_edge_sem, hidden_edge_sem = take(4)
    one_scratch, two_scratch = take(7), take(7)
    first_scratch, second_scratch = take(14), take(14)

    place = Place(groups, dp)
    at, last = place.at, place.last
    _, images, height, channels, width = act.shape
    units = 2 * images
    taps = natural.shape[0]
    depth = taps * channels
    blocks = -(-depth // 128)

    def mine(which):
        flag = jnp.where(owners_ref[which] == at, 1.0, 0.0)
        return jnp.full((1, channels), flag, jnp.float32) > 0.5

    def land_first(k):
        unpack(first.out, natural, k)

        low = k * (depth // fine_chunks) // 128
        high = (k + 1) * (depth // fine_chunks) // 128
        high = jnp.where(k == fine_chunks - 1, blocks, high)

        def one_block(block, carry):
            transform(natural, wide, block)
            return carry

        lax.fori_loop(low, high, one_block, 0)

    def land_second(k):
        unpack(second.out, natural, k)

    first = Stream(
        place, fine_chunks, fine_hop, fine_hop, land_first,
        first_scratch[0], first_scratch[1], first_scratch[2:8], first_scratch[8:],
    )
    second = Stream(
        place, coarse_chunks, coarse_lead, coarse_hop, land_second,
        second_scratch[0], second_scratch[1], second_scratch[2:8], second_scratch[8:],
    )
    one = Renewal(place, mine(0), 0, fine_state, first.col, one_scratch)
    two = Renewal(place, mine(1), 1, coarse_state, second.col, two_scratch)
    x_edges = Edges(
        place, lambda k: x_ref.at[k, 0], lambda k: x_ref.at[k, height - 1],
        lambda side, k: rims.at[0, side, k], x_edge_sem,
    )
    hidden_edges = Edges(
        place, lambda k: act.at[1, k, 0], lambda k: act.at[1, k, height - 1],
        lambda side, k: rims.at[1, side, k], hidden_edge_sem,
    )

    def x_load(k):
        return pltpu.make_async_copy(x_ref.at[k], act.at[0, k], x_sem.at[k])

    def y_store(k):
        return pltpu.make_async_copy(act.at[0, k], y_ref.at[k], y_sem.at[k])

    column = lax.broadcasted_iota(jnp.int32, (16, width), 1)
    not_first = jnp.where(column == 0, 0.0, 1.0).astype(jnp.bfloat16)
    not_last = jnp.where(column == width - 1, 0.0, 1.0).astype(jnp.bfloat16)

    def build(n, patch, e):
        layer, image = n // images, n % images
        lanes = pl.ds(e, 16)
        a = []
        for row in range(-1, height + 1):
            if row < 0:
                v = jnp.where(at > 0, rims[layer, 0, image, lanes].astype(jnp.float32), 0.0)
            elif row == height:
                v = jnp.where(at < dp - 1, rims[layer, 1, image, lanes].astype(jnp.float32), 0.0)
            else:
                v = act[layer, image, row, lanes].astype(jnp.float32)
            a.append(silu(v))
        for q in range(height // rows_out):
            d = a[q * rows_out : q * rows_out + rows_in]
            for j, v in enumerate(spread_rows(d)):
                v = v.astype(jnp.bfloat16)
                before = pltpu.roll(v, 1, 1) * not_first
                after = pltpu.roll(v, width - 1, 1) * not_last
                for tap, part in enumerate((before, v, after)):
                    patch[j, pl.ds(tap * channels + e, 16), q * width : (q + 1) * width] = part

    def settle(n, acc, e):
        layer, image = n // images, n % images
        lanes = pl.ds(e, 16)
        for r, v in enumerate(gather_rows([acc[j, lanes] for j in range(parts)])):
            for q in range(height // rows_out):
                row = q * rows_out + r
                x = act[layer, image, row, lanes].astype(jnp.float32)
                act[1 - layer, image, row, lanes] = (
                    x + v[:, q * width : (q + 1) * width]
                ).astype(jnp.bfloat16)

    slabs = list(range(0, channels, 16))

    def work(n, patch, patch_next, acc, acc_before):
        after, before = jnp.minimum(n + 1, units - 1), jnp.maximum(n - 1, 0)
        for j in range(parts):
            acc[j] = jnp.dot(
                wide[j, :, :depth], patch[j], preferred_element_type=jnp.float32
            )
            for e in slabs[len(slabs) * j // parts : len(slabs) * (j + 1) // parts]:
                build(after, patch_next, e)
                settle(before, acc_before, e)

    fine_steps = pair_hop + Stream.steps(fine_chunks, fine_hop, fine_hop, last)
    coarse_steps = 1 + Stream.steps(coarse_chunks, coarse_lead, coarse_hop, last)
    early = max(coarse_steps - coarse_rate * images, 0)
    total = max(fine_steps, early * coarse_stride, edge_start + edge_stride * images)
    coarse_start = total - early * coarse_stride

    each(fine_chunks, one.start)
    each(images, lambda k: x_load(k).start())
    each(coarse_chunks, two.start)
    place.meet()

    def coarse_step(q):
        at_step(q, coarse_chunks, two.renew)

        def join(k):
            two.join(k)
            second.to_col(k).start()

        at_step(q - 1, coarse_chunks, join)
        second.step(q - 1)

    def join_one(k):
        one.join(k)
        first.to_col(k).start()

    def step(t, carry):
        at_step(t, fine_chunks, one.renew)
        at_step(t - pair_hop, fine_chunks, join_one)
        first.step(t - pair_hop)
        at_stride(t - edge_start, edge_stride, images, x_edges.start)
        at_stride(t - coarse_start, coarse_stride, early, coarse_step)

        @pl.when(t == total - build_back)
        def _():
            x_load(0).wait()
            x_edges.drain(0)
            for e in slabs:
                build(0, patch_0, e)

        return carry

    lax.fori_loop(0, total, step, 0)

    def between(n):
        @pl.when(n < images)
        def _():
            each(coarse_rate, lambda j: coarse_step(early + coarse_rate * n + j))

        @pl.when(n == images)
        def _():
            each(blocks, lambda b: transform(natural, wide, b))

        @pl.when(n + 1 < images)
        def _():
            x_load(n + 1).wait()
            x_edges.drain(n + 1)

        at_step(n + 1 - images, images, hidden_edges.drain)
        at_step(n - 2, images, hidden_edges.start)
        at_step(n - 2 - images, images, lambda k: y_store(k).start())

    def both(t, carry):
        between(2 * t)
        work(2 * t, patch_0, patch_1, acc_0, acc_1)
        between(2 * t + 1)
        work(2 * t + 1, patch_1, patch_0, acc_1, acc_0)
        return carry

    lax.fori_loop(0, images, both, 0)
    y_store(images - 2).start()
    for e in slabs:
        settle(units - 1, acc_1, e)
    y_store(images - 1).start()

    def drain_first(k):
        one.to_pair(k).wait_send()
        first.drain(k)

    def drain_second(k):
        two.to_pair(k).wait_send()
        second.drain(k)

    each(fine_chunks, drain_first)
    each(coarse_chunks, drain_second)
    each(images, lambda k: y_store(k).wait())


def move_kernel(src, dst, held, sem):
    def load(k):
        return pltpu.make_async_copy(src.at[k], held.at[k], sem.at[0, k])

    def store(k):
        return pltpu.make_async_copy(held.at[k], dst.at[k], sem.at[1, k])

    for k in range(src.shape[0]):
        load(k).start()
    for k in range(src.shape[0]):
        load(k).wait()
        store(k).start()
    for k in range(src.shape[0]):
        store(k).wait()


def local(images, kernel_weights, kernel_momentum, kernel_grads, owners):
    groups, dp = lax.axis_size("groups"), lax.axis_size("dp")
    x = images.transpose(0, 1, 3, 2)
    _, _, taps, columns, fan_in, fan_out = kernel_weights.shape
    count, height, channels, width = x.shape
    shares, depth = 2 * groups, columns * fan_in
    padded = -(-depth // 128) * 128
    state = (kernel_weights, kernel_momentum, kernel_grads)

    def cut(chunks):
        return [a.reshape(2, taps, chunks, shares, -1, fan_out) for a in state]

    fine, coarse = depth // fine_chunks // shares, depth // coarse_chunks // shares
    any_space = pl.BlockSpec(memory_space=pl.ANY)
    smem = pl.BlockSpec(memory_space=pltpu.SMEM)
    patch = pltpu.VMEM((parts, depth, height // rows_out * width), jnp.bfloat16)
    acc = pltpu.VMEM((parts, channels, height // rows_out * width), jnp.float32)
    y = pl.pallas_call(
        functools.partial(block_kernel, groups, dp),
        out_shape=jax.ShapeDtypeStruct(x.shape, x.dtype),
        in_specs=[smem] + [any_space] * 7,
        out_specs=any_space,
        scratch_shapes=[
            pltpu.VMEM((2,) + x.shape, x.dtype),
            pltpu.VMEM((2, 2, count, channels, width), x.dtype),
            pltpu.VMEM((taps, padded, fan_out), jnp.float32),
            pltpu.VMEM((parts, fan_out, padded), jnp.bfloat16),
            patch, patch, acc, acc,
            pltpu.SemaphoreType.DMA((count,)),
            pltpu.SemaphoreType.DMA((count,)),
            pltpu.SemaphoreType.DMA((2, 2, count)),
            pltpu.SemaphoreType.DMA((2, 2, count)),
        ]
        + Renewal.scratch(fine_chunks, taps, fine, fan_out)
        + Renewal.scratch(coarse_chunks, taps, coarse, fan_out)
        + Stream.scratch(fine_chunks, taps * fine, fan_out, groups)
        + Stream.scratch(coarse_chunks, taps * coarse, fan_out, groups),
        compiler_params=pltpu.CompilerParams(
            collective_id=0, has_side_effects=True, vmem_limit_bytes=60 << 20
        ),
    )(owners, *cut(fine_chunks), *cut(coarse_chunks), x)
    y = pl.pallas_call(
        move_kernel,
        out_shape=jax.ShapeDtypeStruct(x.shape, x.dtype),
        in_specs=[any_space],
        out_specs=any_space,
        scratch_shapes=[
            pltpu.VMEM(x.shape, x.dtype),
            pltpu.SemaphoreType.DMA((2, count)),
        ],
    )(y)
    return y.transpose(0, 1, 3, 2)


def solution(mesh):
    placed = (
        P("groups", "dp", None, None),
        P("dp", None, None, None, None, None),
        P("dp", None, None, None, None, None),
        P("dp", None, None, None, None, None),
        P(),
    )
    return jax.shard_map(
        local, mesh=mesh, in_specs=placed, out_specs=P("groups", "dp", None, None), check_vma=False
    )
```
